32 devices in a mesh: layer: 4 (over y, core), row: 8 (over z, x).
Axes of the slice: x: 2, y: 2, z: 4, core: 2. Of those that a mesh axis runs over, the one named last changes fastest.
Arguments:
- transmission: bfloat16 [4, 6144, 6144], P('layer', 'row'), may hold values from -0.078125 to 0.078125
- reflection: bfloat16 [4, 6144, 6144], P('layer', 'row'), may hold values from -0.078125 to 0.078125
- receiver_map: bfloat16 [4, 6144, 6144], P('layer', 'row'), may hold values from -0.078125 to 0.078125
- midplane_map: bfloat16 [4, 6144, 6144], P('layer', 'row'), may hold values from -0.078125 to 0.078125
- traces: bfloat16 [4, 6144, 384], P('layer', 'row'), may hold values from -6 to 6
- sources: bfloat16 [4, 3, 6144, 384], P('layer', None, 'row'), may hold values from -5 to 5
Outputs:
- reflected: bfloat16 [4, 3, 6144, 384], P('layer', None, 'row')
- recorded: bfloat16 [4, 3, 6144, 384], P('layer', None, 'row')
- midfield: bfloat16 [4, 3, 6144, 384], P('layer', None, 'row')
- transmitted: bfloat16 [4, 6144, 384], P('layer', 'row')
The draws below stay inside these ranges and needn't reach their ends.
All inputs are finite; a program needn't handle non-finite values.
Results may differ from the reference program's by a relative error of at most 0.0052.
Values may be sent and summed in bfloat16 or wider, within the bound.
No kernel may reach another device: no remote copies, remote signals or barrier semaphores. Data moves between devices by JAX's collectives and lax.ppermute only.
A program may use at most 128 MiB of HBM per device.

```python
import jax
import jax.numpy as jnp
from jax import lax

M = 6144
B = 384
TICKS = 3
SECTIONS = 4


def level_of(own_key, shape, shards, smallest, top_value):
    gain, own = 1.0, jax.random.fold_in(own_key, 6)
    for position, parts in shards:
        steps = jnp.exp(jax.random.uniform(jax.random.fold_in(own, position), (parts,), jnp.float32, smallest / len(shards), top_value / len(shards)))
        gain = gain * jnp.repeat(steps, shape[position] // parts).reshape([-1 if axis == position else 1 for axis in range(len(shape))])
    return gain


def bell_draw(rng, extent, width, bound, shards=(), kind=jnp.bfloat16):
    drawn = jax.random.normal(rng, extent, jnp.float32) * width
    if len(shards) > 0:
        drawn = level_of(rng, extent, shards, -0.22, 0.18) * drawn
    return jnp.clip(drawn, min=-bound, max=bound).astype(kind)


def setup_inputs(seed: int = 0) -> dict:
    arg_keys = jax.random.split(jax.random.key(seed), 7)
    transmission = bell_draw(arg_keys[0], (SECTIONS, M, M), M ** -0.5, 0.078125, ((0, 4), (1, 8)))
    reflection = bell_draw(arg_keys[1], (SECTIONS, M, M), M ** -0.5, 0.078125, ((0, 4), (1, 8)))
    receiver_map = bell_draw(arg_keys[2], (SECTIONS, M, M), M ** -0.5, 0.078125, ((0, 4), (1, 8)))
    midplane_map = bell_draw(arg_keys[3], (SECTIONS, M, M), M ** -0.5, 0.078125, ((0, 4), (1, 8)))
    traces = bell_draw(arg_keys[4], (SECTIONS, M, B), 1.0, 6.0, ((0, 4), (1, 8)))
    sources = bell_draw(arg_keys[5], (SECTIONS, TICKS, M, B), 0.7, 5.0, ((0, 4), (2, 8)))
    return dict(transmission=transmission, reflection=reflection, receiver_map=receiver_map, midplane_map=midplane_map, traces=traces, sources=sources)


def one_section(operands):
    transmit_rows, reflect_rows, receive_rows, middle_rows, incoming, source_now = operands
    sent = jnp.dot(transmit_rows, incoming, preferred_element_type=jnp.float32) + source_now.astype(jnp.float32)
    bounced = jnp.dot(reflect_rows, incoming, preferred_element_type=jnp.float32)
    heard = jnp.dot(receive_rows, incoming, preferred_element_type=jnp.float32)
    middle = jnp.dot(middle_rows, incoming, preferred_element_type=jnp.float32)
    return (sent.astype(jnp.bfloat16), bounced.astype(jnp.bfloat16),
            heard.astype(jnp.bfloat16), middle.astype(jnp.bfloat16))


def reference(transmission, reflection, receiver_map, midplane_map, traces, sources):
    incoming = traces
    bounced_all = []
    heard_all = []
    middle_all = []
    sent = traces
    for tick in range(TICKS):
        sent, bounced, heard, middle = lax.map(one_section, (transmission, reflection, receiver_map, midplane_map, incoming, sources[:, tick]))
        bounced_all.append(bounced)
        heard_all.append(heard)
        middle_all.append(middle)
        incoming = jnp.concatenate([jnp.zeros((1, M, B), jnp.bfloat16), sent[:-1]], axis=0)
    return (jnp.stack(bounced_all, axis=1), jnp.stack(heard_all, axis=1),
            jnp.stack(middle_all, axis=1), sent)
```

```python
import functools

import jax
import jax.numpy as jnp
import numpy as np
from jax import lax
from jax.experimental import pallas as pl
from jax.experimental.pallas import tpu as pltpu
from jax.sharding import PartitionSpec as P

ANY = pl.BlockSpec(memory_space=pl.ANY)
SMEM = pl.BlockSpec(memory_space=pltpu.SMEM)


def ring_order(n):
    return list(range(0, n, 2)) + list(range(n - 1, 0, -2))


def owner_table(n):
    order = ring_order(n)
    table = np.zeros((n, n), np.int32)
    for place, r in enumerate(order):
        offsets = [0]
        for s in range(1, n // 2 + 1):
            offsets += [-s, s] if 2 * s < n else [-s]
        for j, o in enumerate(offsets):
            table[r, j] = order[(place + o) % n]
    return table


def ring_hop(x, n, by):
    order = ring_order(n)
    return lax.ppermute(x, "row", [(order[i], order[(i + by) % n]) for i in range(n)])


def accumulate_kernel(places, offsets, carried, finish, tick, own, *refs):
    mats, parts = len(finish), len(places)
    refs = list(refs)
    take = lambda count: [refs.pop(0) for _ in range(count)]
    weights, shards = take(mats), take(parts)
    carry_in = take(mats) if carried else []
    src = take(1)[0] if "send" in finish else None
    sizes = [s.shape[0] for s in shards]
    starts = [sum(sizes[:i]) for i in range(parts)]
    n_out = sum(2 if f == "send" else 1 for f in finish)
    while len(refs) > n_out + 9:
        refs.pop(0)
    outs = take(n_out)
    wbuf, xbuf, acc, stage, xsem, wsem, asem, osem, ssem = refs
    depth = weights[0].shape[1] // (own.shape[1] - 1)
    x_in = [pltpu.make_async_copy(shards[i], xbuf.at[pl.ds(starts[i], sizes[i])], xsem.at[i])
            for i in range(parts)]
    for c in x_in:
        c.start()
    w_in, a_in = [], []
    for m in range(mats):
        row = []
        for i in range(parts):
            first = own[0, places[i]] * depth + offsets[i]
            columns = pl.ds(pl.multiple_of(first, 128), sizes[i])
            row.append(pltpu.make_async_copy(
                weights[m].at[:, columns], wbuf.at[m, :, pl.ds(starts[i], sizes[i])],
                wsem.at[m * parts + i]))
            row[-1].start()
        w_in.append(row)
        if carried:
            a_in.append(pltpu.make_async_copy(carry_in[m], acc.at[m], asem.at[m]))
            a_in[-1].start()
        if finish[m] == "send":
            src_in = pltpu.make_async_copy(src.at[0, tick], stage.at[mats], ssem)
            src_in.start()
    for c in x_in:
        c.wait()
    pending, sem = [], 0
    for m in range(mats):
        for c in w_in[m]:
            c.wait()
        product = jnp.dot(wbuf[m], xbuf[...], preferred_element_type=jnp.float32)
        if carried:
            a_in[m].wait()
            acc[m] = acc[m] + product
        else:
            acc[m] = product
        if finish[m] == "carry":
            copies = [(acc.at[m], outs.pop(0))]
        elif finish[m] == "emit":
            stage[m] = acc[m].astype(stage.dtype)
            copies = [(stage.at[m], outs.pop(0).at[0, tick])]
        else:
            src_in.wait()
            sent = acc[m] + stage[mats].astype(jnp.float32)
            stage[m] = sent.astype(stage.dtype)
            stage[mats] = (sent * own[0, own.shape[1] - 1].astype(jnp.float32)).astype(stage.dtype)
            copies = [(stage.at[mats], outs.pop(0)), (stage.at[m], outs.pop(0))]
        for a, b in copies:
            pending.append(pltpu.make_async_copy(a, b, osem.at[sem]))
            pending[-1].start()
            sem += 1
    for c in pending:
        c.wait()


def accumulate(own, weights, parts, carry, finish, tick, sources, held):
    mats, (rows, unknowns) = len(weights), weights[0].shape
    cols = parts[0][0].shape[1]
    depth = sum(p[0].shape[0] for p in parts)
    args = [own, *weights, *[p[0] for p in parts], *(carry or [])]
    if "send" in finish:
        args.append(sources)
    shapes, aliases = [], {}
    for m, f in enumerate(finish):
        if f == "carry":
            shapes.append(jax.ShapeDtypeStruct((rows, cols), jnp.float32))
        elif f == "emit":
            if held[m] is not None:
                aliases[len(args)] = len(shapes)
                args.append(held[m])
            shapes.append(jax.ShapeDtypeStruct((1, sources.shape[1], rows, cols), jnp.bfloat16))
        else:
            shapes += [jax.ShapeDtypeStruct((rows, cols), jnp.bfloat16)] * 2
    return pl.pallas_call(
        functools.partial(
            accumulate_kernel, tuple(p[1] for p in parts), tuple(p[2] for p in parts),
            bool(carry), tuple(finish), tick),
        out_shape=tuple(shapes),
        in_specs=[SMEM] + [ANY] * (len(args) - 1),
        out_specs=tuple(ANY for _ in shapes),
        input_output_aliases=aliases,
        scratch_shapes=[
            pltpu.VMEM((mats, rows, depth), jnp.bfloat16),
            pltpu.VMEM((depth, cols), jnp.bfloat16),
            pltpu.VMEM((mats, rows, cols), jnp.float32),
            pltpu.VMEM((mats + 1, rows, cols), jnp.bfloat16),
            pltpu.SemaphoreType.DMA((len(parts),)),
            pltpu.SemaphoreType.DMA((len(parts) * mats,)),
            pltpu.SemaphoreType.DMA((mats,)),
            pltpu.SemaphoreType.DMA((mats + 1,)),
            pltpu.SemaphoreType.DMA,
        ],
        compiler_params=pltpu.CompilerParams(vmem_limit_bytes=62 << 20),
        cost_estimate=pl.CostEstimate(
            flops=2 * mats * rows * depth * 512, bytes_accessed=2 * mats * rows * depth,
            transcendentals=0),
    )(*args)


def sweep(layers, n, transmission, reflection, receiver_map, midplane_map, traces, sources):
    ticks = sources.shape[1]
    weights = [transmission[0], reflection[0], receiver_map[0], midplane_map[0]]
    row = lax.dynamic_slice_in_dim(jnp.asarray(owner_table(n)), lax.axis_index("row"), 1, 0)
    passes_on = jnp.where(lax.axis_index("layer") < layers - 1, 1, 0).astype(jnp.int32)
    own = jnp.concatenate([row, passes_on.reshape(1, 1)], axis=1)
    outs = [None] * 3
    incoming = traces[0]
    half = incoming.shape[0] // 2
    around = [(i, (i + 1) % layers) for i in range(layers)]
    last_step = n // 2
    left_over = None

    for tick in range(ticks):
        final = tick + 1 == ticks
        up = down = incoming
        ready = [(incoming, 0, 0)]
        carry = None
        for s in range(1, last_step + 1):
            if s < last_step:
                new_up = ring_hop(up, n, 1)
                new_down = ring_hop(down, n, -1)
                arrived = [(new_up, 2 * s - 1, 0), (new_down, 2 * s, 0)]
            else:
                new_up = ring_hop(up[:half], n, 1)
                new_down = ring_hop(down[half:], n, -1)
                arrived = [(new_up, n - 1, 0), (new_down, n - 1, half)]
            if s == 1:
                if left_over is not None:
                    outs = list(accumulate(own, weights[1:], *left_over, ["emit"] * 3, tick - 1, sources,
                                    outs))
            elif s < last_step or final:
                carry = list(accumulate(own, weights, ready, carry, ["carry"] * 4, tick, sources, None))
                ready = []
            else:
                sums = accumulate(own, weights[:1], ready, carry[:1], ["carry"], tick, sources, None)
                carry = list(sums) + carry[1:]
            ready = ready + arrived
            up, down = new_up, new_down
        if final:
            res = accumulate(own, weights, ready, carry, ["send"] + ["emit"] * 3, tick, sources,
                      [None] + outs)
            return res[2], res[3], res[4], res[1][None]
        passed, _ = accumulate(own, weights[:1], arrived, carry[:1], ["send"], tick, sources, None)
        left_over = (ready, carry[1:])
        incoming = lax.ppermute(passed, "layer", around)


def plain_program(layers, transmission, reflection, receiver_map, midplane_map, traces, sources):
    incoming = sent = traces[0]
    outs = [[], [], []]
    for tick in range(sources.shape[1]):
        piece = lax.all_gather(incoming, "row", axis=0, tiled=True)
        total = jnp.dot(transmission[0], piece, preferred_element_type=jnp.float32)
        sent = (total + sources[0, tick].astype(jnp.float32)).astype(jnp.bfloat16)
        for out, w in zip(outs, (reflection, receiver_map, midplane_map)):
            out.append(jnp.dot(w[0], piece, preferred_element_type=jnp.float32).astype(jnp.bfloat16))
        incoming = lax.ppermute(sent, "layer", [(i, i + 1) for i in range(layers - 1)])
    return tuple(jnp.stack(o)[None] for o in outs) + (sent[None],)


def solution(mesh):
    layers, n = mesh.shape["layer"], mesh.shape["row"]

    def body(transmission, reflection, receiver_map, midplane_map, traces, sources):
        args = (transmission, reflection, receiver_map, midplane_map, traces, sources)
        if traces.shape[1] % 256 or n % 2 or n < 4:
            return plain_program(layers, *args)
        return sweep(layers, n, *args)

    wide = P("layer", "row", None)
    deep = P("layer", None, "row", None)
    return jax.shard_map(
        body,
        mesh=mesh,
        in_specs=(wide, wide, wide, wide, wide, deep),
        out_specs=(deep, deep, deep, wide),
        check_vma=False,
    )
```

```python
import functools

import jax
import jax.numpy as jnp
import numpy as np
from jax import lax
from jax.experimental import pallas as pl
from jax.experimental.pallas import tpu as pltpu
from jax.sharding import PartitionSpec as P

ANY = pl.BlockSpec(memory_space=pl.ANY)
VMEM = pl.BlockSpec(memory_space=pltpu.VMEM)
SMEM = pl.BlockSpec(memory_space=pltpu.SMEM)


def ring_order(n):
    return list(range(0, n, 2)) + list(range(n - 1, 0, -2))


def owner_table(n):
    order = ring_order(n)
    table = np.zeros((n, n), np.int32)
    for place, r in enumerate(order):
        offsets = [0]
        for s in range(1, n // 2 + 1):
            offsets += [-s, s] if 2 * s < n else [-s]
        for j, o in enumerate(offsets):
            table[r, j] = order[(place + o) % n]
    return table


def ring_hop(x, n, by):
    order = ring_order(n)
    return lax.ppermute(x, "row", [(order[i], order[(i + by) % n]) for i in range(n)])


def accumulate_kernel(places, offsets, sums_in, first, finish, tick, blocks, own, *refs):
    mats, parts = len(finish), len(places)
    refs = list(refs)
    take = lambda count: [refs.pop(0) for _ in range(count)]
    weights, shards = take(mats), take(parts)
    carry_in = take(1)[0] if sums_in else None
    src = take(1)[0] if "sourced" in finish else None
    stage, osem, ssem = refs[-3:]
    keeps = not {"carry", "sourced"}.isdisjoint(finish)
    n_out = sum(f in ("emit", "send") for f in finish) + keeps
    outs = refs[-3 - n_out:-3]
    carry_out = outs.pop(0) if keeps else None
    rows, unknowns = weights[0].shape
    depth = unknowns // own.shape[1]
    height = rows // blocks
    if src is not None:
        src_in = pltpu.make_async_copy(src.at[0, tick], stage.at[0], ssem)
        src_in.start()
        src_in.wait()
    columns = [
        pl.ds(pl.multiple_of(own[0, places[i]] * depth + offsets[i], 128), shards[i].shape[0])
        for i in range(parts)]

    def block(r, carry):
        lines = pl.ds(pl.multiple_of(r * height, height), height)
        for m in range(mats):
            total = carry_in[first + m, lines, :] if sums_in else None
            for i in range(parts):
                product = jnp.dot(weights[m][lines, columns[i]], shards[i][...],
                                  preferred_element_type=jnp.float32)
                total = product if total is None else total + product
            if finish[m] == "sourced":
                total = total + stage[0, lines, :].astype(jnp.float32)
            if finish[m] in ("carry", "sourced"):
                carry_out[first + m, lines, :] = total
            elif finish[m] == "emit":
                stage[m, lines, :] = total.astype(stage.dtype)
            else:
                outs[m][lines, :] = total.astype(stage.dtype)
        return carry

    lax.fori_loop(0, blocks, block, 0)
    pending = [(stage.at[m], outs[m].at[0, tick]) for m in range(mats) if finish[m] == "emit"]
    pending = [pltpu.make_async_copy(a, b, osem.at[k]) for k, (a, b) in enumerate(pending)]
    for c in pending:
        c.start()
    for c in pending:
        c.wait()


def in_vmem(x):
    return pltpu.with_memory_space_constraint(x, pltpu.VMEM)


def in_hbm(x):
    return pltpu.with_memory_space_constraint(x, pltpu.HBM)


def accumulate(own, weights, parts, carry, first, finish, tick, sources, held):
    mats, (rows, unknowns) = len(weights), weights[0].shape
    cols = parts[0][0].shape[1]
    depth = sum(p[0].shape[0] for p in parts)
    args = [own, *[in_vmem(w) for w in weights], *[in_vmem(p[0]) for p in parts]]
    specs = [SMEM] + [VMEM] * (len(args) - 1)
    shapes, out_specs, aliases = [], [], {}
    if not {"carry", "sourced"}.isdisjoint(finish):
        shapes.append(jax.ShapeDtypeStruct((4, rows, cols), jnp.float32))
        out_specs.append(VMEM)
        if carry is not None:
            aliases[len(args)] = 0
    if carry is not None:
        args.append(in_vmem(carry))
        specs.append(VMEM)
    if "sourced" in finish:
        args.append(in_hbm(sources))
        specs.append(ANY)
    for m, f in enumerate(finish):
        if f == "emit":
            if held[m] is not None:
                aliases[len(args)] = len(shapes)
                args.append(in_hbm(held[m]))
                specs.append(ANY)
            shapes.append(jax.ShapeDtypeStruct((1, sources.shape[1], rows, cols), jnp.bfloat16))
            out_specs.append(ANY)
        elif f == "send":
            shapes.append(jax.ShapeDtypeStruct((rows, cols), jnp.bfloat16))
            out_specs.append(VMEM)
    stages = mats if "emit" in finish else 1
    return pl.pallas_call(
        functools.partial(
            accumulate_kernel, tuple(p[1] for p in parts), tuple(p[2] for p in parts),
            carry is not None, first, tuple(finish), tick, 2),
        out_shape=tuple(shapes),
        in_specs=specs,
        out_specs=tuple(out_specs),
        input_output_aliases=aliases,
        scratch_shapes=[
            pltpu.VMEM((stages, rows, cols), jnp.bfloat16),
            pltpu.SemaphoreType.DMA((mats + 1,)),
            pltpu.SemaphoreType.DMA,
        ],
        compiler_params=pltpu.CompilerParams(vmem_limit_bytes=(2 << 20) + stages * rows * cols * 2),
        cost_estimate=pl.CostEstimate(
            flops=2 * mats * rows * depth * 512, bytes_accessed=2 * mats * rows * depth,
            transcendentals=0),
    )(*args)


def load_kernel(own, *refs):
    mats = (len(refs) - 3) // 2
    weights, x, held, carry, sem = refs[:mats], refs[mats], refs[mats + 1:-2], refs[-2], refs[-1]
    depth = x.shape[0]
    copies = [pltpu.make_async_copy(weights[m], held[m], sem.at[m]) for m in range(mats)]
    copies[0].start()
    columns = pl.ds(pl.multiple_of(own[0, 0] * depth, 128), depth)
    for m in range(mats):
        if m + 1 < mats:
            copies[m + 1].start()
        copies[m].wait()
        carry[m] = jnp.dot(held[m][:, columns], x[...], preferred_element_type=jnp.float32)


def load(own, weights, x):
    mats, (rows, unknowns) = len(weights), weights[0].shape
    held = [jax.ShapeDtypeStruct(w.shape, w.dtype) for w in weights]
    res = pl.pallas_call(
        load_kernel,
        out_shape=(*held, jax.ShapeDtypeStruct((mats, rows, x.shape[1]), jnp.float32)),
        in_specs=[SMEM] + [ANY] * mats + [VMEM],
        out_specs=(VMEM,) * (mats + 1),
        scratch_shapes=[pltpu.SemaphoreType.DMA((mats,))],
        compiler_params=pltpu.CompilerParams(vmem_limit_bytes=2 << 20),
        cost_estimate=pl.CostEstimate(
            flops=2 * mats * rows * x.shape[0] * 512, bytes_accessed=4 * mats * rows * unknowns,
            transcendentals=0),
    )(own, *[in_hbm(w) for w in weights], in_vmem(x))
    return res[:mats], res[mats]


def sweep(layers, n, transmission, reflection, receiver_map, midplane_map, traces, sources):
    ticks = sources.shape[1]
    weights = [transmission[0], reflection[0], receiver_map[0], midplane_map[0]]
    own = lax.dynamic_slice_in_dim(jnp.asarray(owner_table(n)), lax.axis_index("row"), 1, 0)
    outs = [None] * 3
    incoming = traces[0]
    half = incoming.shape[0] // 2
    last_step = n // 2
    late = None

    def multiply(which, parts, carry, finish, tick, held=None):
        return accumulate(own, [weights[i] for i in which], parts, carry, which[0], finish, tick,
                          sources, held)

    for tick in range(ticks):
        final = tick + 1 == ticks
        up = down = incoming
        ready = [(incoming, 0, 0)]
        carry = None if tick == 0 else carry
        for s in range(1, last_step + 1):
            if s < last_step:
                new_up = ring_hop(up, n, 1)
                new_down = ring_hop(down, n, -1)
                arrived = [(new_up, 2 * s - 1, 0), (new_down, 2 * s, 0)]
            else:
                new_up = ring_hop(up[:half], n, 1)
                new_down = ring_hop(down[half:], n, -1)
                arrived = [(new_up, n - 1, 0), (new_down, n - 1, half)]
            if s == 1:
                if tick == 0:
                    weights, carry = load(own, weights, incoming)
                    ready = []
                else:
                    outs = list(multiply((1, 2, 3), late, carry, ["emit"] * 3, tick - 1, outs))
                    carry = None
            else:
                source = "sourced" if s == last_step else "carry"
                if s < last_step or final:
                    carry = multiply((0, 1, 2, 3), ready, carry, [source] + ["carry"] * 3, tick)[0]
                    late = []
                else:
                    carry = multiply((0,), ready, carry, [source], tick)[0]
                    late = ready
                ready = []
            ready = ready + arrived
            up, down = new_up, new_down
        if final:
            res = multiply((0, 1, 2, 3), ready, carry, ["send"] + ["emit"] * 3, tick,
                           [None] + outs)
            return res[1], res[2], res[3], res[0][None]
        sent = multiply((0,), ready, carry, ["send"], tick)[0]
        late = late + ready
        incoming = lax.ppermute(sent, "layer", [(i, i + 1) for i in range(layers - 1)])


def plain_program(layers, transmission, reflection, receiver_map, midplane_map, traces, sources):
    incoming = sent = traces[0]
    outs = [[], [], []]
    for tick in range(sources.shape[1]):
        piece = lax.all_gather(incoming, "row", axis=0, tiled=True)
        total = jnp.dot(transmission[0], piece, preferred_element_type=jnp.float32)
        sent = (total + sources[0, tick].astype(jnp.float32)).astype(jnp.bfloat16)
        for out, w in zip(outs, (reflection, receiver_map, midplane_map)):
            out.append(jnp.dot(w[0], piece, preferred_element_type=jnp.float32).astype(jnp.bfloat16))
        incoming = lax.ppermute(sent, "layer", [(i, i + 1) for i in range(layers - 1)])
    return tuple(jnp.stack(o)[None] for o in outs) + (sent[None],)


def solution(mesh):
    layers, n = mesh.shape["layer"], mesh.shape["row"]

    def body(transmission, reflection, receiver_map, midplane_map, traces, sources):
        args = (transmission, reflection, receiver_map, midplane_map, traces, sources)
        if traces.shape[1] % 256 or n % 2 or n < 4:
            return plain_program(layers, *args)
        return sweep(layers, n, *args)

    wide = P("layer", "row", None)
    deep = P("layer", None, "row", None)
    return jax.shard_map(
        body,
        mesh=mesh,
        in_specs=(wide, wide, wide, wide, wide, deep),
        out_specs=(deep, deep, deep, wide),
        check_vma=False,
    )
```

```python
import functools

import jax
import jax.numpy as jnp
import numpy as np
from jax import lax
from jax.experimental import pallas as pl
from jax.experimental.pallas import tpu as pltpu
from jax.sharding import PartitionSpec as P

ANY = pl.BlockSpec(memory_space=pl.ANY)
VMEM = pl.BlockSpec(memory_space=pltpu.VMEM)
SMEM = pl.BlockSpec(memory_space=pltpu.SMEM)
KEPT = 3


def ring_order(n):
    return list(range(0, n, 2)) + list(range(n - 1, 0, -2))


def owner_table(n):
    order = ring_order(n)
    table = np.zeros((2, n, n), np.int32)
    for parity, sign in enumerate((1, -1)):
        for place, r in enumerate(order):
            offsets = [0]
            for s in range(1, n // 2 + 1):
                offsets += [-s, s] if 2 * s < n else [-s]
            for j, o in enumerate(offsets):
                table[parity, r, j] = order[(place + sign * o) % n]
    return table


def ring_hop(x, layers, n, by):
    order = ring_order(n)
    pairs = []
    for layer in range(layers):
        step = by if layer % 2 == 0 else -by
        pairs += [(layer * n + order[i], layer * n + order[(i + step) % n]) for i in range(n)]
    return lax.ppermute(x, ("layer", "row"), pairs)


def accumulate_kernel(places, counts, sums_in, first, finish, tick, blocks, own, *refs):
    mats, parts = len(finish), len(places)
    refs = list(refs)
    take = lambda count: [refs.pop(0) for _ in range(count)]
    weights, pieces = take(mats), [take(c) for c in counts]
    carry_in = take(1)[0] if sums_in else None
    src = take(1)[0] if "sourced" in finish else None
    xbuf, stage, wbuf, osem, ssem, wsem = refs[-6:]
    streamed = first + mats > KEPT
    keeps = not {"carry", "sourced"}.isdisjoint(finish)
    n_out = sum({"emit": 1, "send": 1, "split": len(cuts_of(stage.shape[1]))}.get(f, 0) for f in finish) + keeps
    outs = refs[-6 - n_out:-6]
    carry_out = outs.pop(0) if keeps else None
    rows, unknowns = weights[0].shape
    depth = unknowns // own.shape[1]
    height = rows // blocks
    columns = [pl.ds(pl.multiple_of(own[0, p] * depth, 128), depth) for p in places]
    if streamed:
        w_in = [pltpu.make_async_copy(weights[-1].at[:, columns[i]], wbuf.at[i], wsem.at[i])
                for i in range(parts)]
        for c in w_in:
            c.start()
    if src is not None:
        src_in = pltpu.make_async_copy(src.at[0, tick], stage.at[0], ssem)
        src_in.start()
    for i in range(parts):
        at = 0
        for piece in pieces[i]:
            xbuf[i, at:at + piece.shape[0], :] = piece[...]
            at += piece.shape[0]
    if src is not None:
        src_in.wait()

    def block(r, m):
        lines = pl.ds(pl.multiple_of(r * height, height), height)
        total = carry_in[first + m, lines, :] if sums_in else None
        for i in range(parts):
            rhs = wbuf[i, lines, :] if first + m >= KEPT else weights[m][lines, columns[i]]
            product = jnp.dot(rhs, xbuf[i], preferred_element_type=jnp.float32)
            total = product if total is None else total + product
        if finish[m] == "sourced":
            total = total + stage[0, lines, :].astype(jnp.float32)
        if finish[m] in ("carry", "sourced"):
            carry_out[first + m, lines, :] = total
        elif finish[m] == "send":
            outs[m][lines, :] = total.astype(stage.dtype)
        else:
            stage[m, lines, :] = total.astype(stage.dtype)

    def blocks_of(held):
        def body(r, carry):
            for m in held:
                block(r, m)
            return carry

        lax.fori_loop(0, blocks, body, 0)

    emitting = [None] * mats

    def emit(m):
        if finish[m] == "emit":
            emitting[m] = pltpu.make_async_copy(stage.at[m], outs[m].at[0, tick], osem.at[m])
            emitting[m].start()

    kept = mats - streamed
    if "emit" in finish:
        for m in range(kept):
            blocks_of([m])
            emit(m)
    else:
        blocks_of(range(kept))
    if streamed:
        for c in w_in:
            c.wait()
        blocks_of([kept])
        emit(kept)
    if finish[0] == "split":
        at = 0
        for out in outs:
            out[...] = stage[0, at:at + out.shape[0], :]
            at += out.shape[0]
    for c in emitting:
        if c is not None:
            c.wait()


def cuts_of(rows):
    return rows // 2, rows - rows // 2


def in_vmem(x):
    return pltpu.with_memory_space_constraint(x, pltpu.VMEM)


def in_hbm(x):
    return pltpu.with_memory_space_constraint(x, pltpu.HBM)


def accumulate(own, weights, parts, carry, first, finish, tick, sources, held):
    mats, (rows, unknowns) = len(finish), weights[0].shape
    cols = parts[0][0][0].shape[1]
    deep = unknowns // own.shape[1]
    depth = len(parts) * deep
    held_here = [first + m < KEPT for m in range(mats)]
    xs = [in_vmem(x) for p in parts for x in p[0]]
    args = [own, *[in_vmem(w) if h else in_hbm(w) for w, h in zip(weights, held_here)], *xs]
    specs = [SMEM] + [VMEM if h else ANY for h in held_here] + [VMEM] * len(xs)
    shapes, out_specs, aliases = [], [], {}
    if not {"carry", "sourced"}.isdisjoint(finish):
        shapes.append(jax.ShapeDtypeStruct((4, rows, cols), jnp.float32))
        out_specs.append(VMEM)
        if carry is not None:
            aliases[len(args)] = 0
    if carry is not None:
        args.append(in_vmem(carry))
        specs.append(VMEM)
    if "sourced" in finish:
        args.append(in_hbm(sources))
        specs.append(ANY)
    for m, f in enumerate(finish):
        if f == "emit":
            if held[m] is not None:
                aliases[len(args)] = len(shapes)
                args.append(in_hbm(held[m]))
                specs.append(ANY)
            shapes.append(jax.ShapeDtypeStruct((1, sources.shape[1], rows, cols), jnp.bfloat16))
            out_specs.append(ANY)
        elif f in ("send", "split"):
            for height in (rows,) if f == "send" else cuts_of(rows):
                shapes.append(jax.ShapeDtypeStruct((height, cols), jnp.bfloat16))
                out_specs.append(VMEM)
    streams = 1 if all(held_here) else len(parts)
    small = 0 if all(held_here) else streams * rows * deep * 2
    stages = mats if "emit" in finish else 1
    return pl.pallas_call(
        functools.partial(
            accumulate_kernel, tuple(p[1] for p in parts), tuple(len(p[0]) for p in parts),
            carry is not None, first, tuple(finish), tick, 2),
        out_shape=tuple(shapes),
        in_specs=specs,
        out_specs=tuple(out_specs),
        input_output_aliases=aliases,
        scratch_shapes=[
            pltpu.VMEM((len(parts), deep, cols), jnp.bfloat16),
            pltpu.VMEM((stages, rows, cols), jnp.bfloat16),
            pltpu.VMEM((streams, rows, deep) if small else (1, 8, 128), jnp.bfloat16),
            pltpu.SemaphoreType.DMA((mats + 1,)),
            pltpu.SemaphoreType.DMA,
            pltpu.SemaphoreType.DMA((streams,)),
        ],
        compiler_params=pltpu.CompilerParams(vmem_limit_bytes=(2 << 20) + (stages * rows + depth) * cols * 2 + small),
        cost_estimate=pl.CostEstimate(
            flops=2 * mats * rows * depth * 512, bytes_accessed=2 * mats * rows * depth,
            transcendentals=0),
    )(*args)


def load_kernel(own, *refs):
    mats = 4
    weights, x, rest = refs[:mats], refs[mats], refs[mats + 1:]
    held, (carry, wbuf, sem) = rest[:KEPT], rest[KEPT:]
    depth = x.shape[0]
    columns = pl.ds(pl.multiple_of(own[0, 0] * depth, 128), depth)
    copies = [pltpu.make_async_copy(weights[m], held[m], sem.at[m]) for m in range(KEPT)]
    copies.append(pltpu.make_async_copy(weights[KEPT].at[:, columns], wbuf, sem.at[KEPT]))
    copies[0].start()
    for m in range(mats):
        if m + 1 < mats:
            copies[m + 1].start()
        copies[m].wait()
        block = held[m][:, columns] if m < KEPT else wbuf[...]
        carry[m] = jnp.dot(block, x[...], preferred_element_type=jnp.float32)


def load(own, weights, x):
    mats, (rows, unknowns) = len(weights), weights[0].shape
    depth, cols = x.shape
    *held, carry = pl.pallas_call(
        load_kernel,
        out_shape=(*[jax.ShapeDtypeStruct(w.shape, w.dtype) for w in weights[:KEPT]],
                   jax.ShapeDtypeStruct((mats, rows, cols), jnp.float32)),
        in_specs=[SMEM] + [ANY] * mats + [VMEM],
        out_specs=(VMEM,) * (KEPT + 1),
        scratch_shapes=[pltpu.VMEM((rows, depth), jnp.bfloat16),
                        pltpu.SemaphoreType.DMA((mats,))],
        compiler_params=pltpu.CompilerParams(vmem_limit_bytes=(2 << 20) + 2 * rows * depth),
        cost_estimate=pl.CostEstimate(
            flops=2 * mats * rows * depth * 512, bytes_accessed=4 * mats * rows * unknowns,
            transcendentals=0),
    )(own, *[in_hbm(w) for w in weights], in_vmem(x))
    return [*held, *weights[KEPT:]], carry


def sweep(layers, n, transmission, reflection, receiver_map, midplane_map, traces, sources):
    ticks = sources.shape[1]
    weights = [transmission[0], reflection[0], receiver_map[0], midplane_map[0]]
    own = lax.dynamic_slice(
        jnp.asarray(owner_table(n)),
        (lax.axis_index("layer") % 2, lax.axis_index("row"), 0), (1, 1, n))[0]
    outs = [None] * 3
    incoming = [traces[0]]
    last_step = n // 2
    late = carry = None

    def multiply(which, parts, carry, finish, tick, held=None):
        return accumulate(own, [weights[i] for i in which], parts, carry, which[0], finish, tick,
                          sources, held)

    for tick in range(ticks):
        final = tick + 1 == ticks
        streams = range(len(incoming))
        ups, downs = list(incoming), list(incoming)
        ready = [(incoming, 0)]
        for s in range(1, last_step + 1):
            hop = lambda x, by: ring_hop(x, layers, n, by)
            if s < last_step:
                for c in streams:
                    ups[c], downs[c] = hop(ups[c], 1), hop(downs[c], -1)
                arrived = [(list(ups), 2 * s - 1), (list(downs), 2 * s)]
            else:
                arrived = [([hop((ups, downs)[c][c], 1 - 2 * c) for c in streams], n - 1)]
            if s == 1 and tick == 0:
                weights, carry = load(own, weights, traces[0])
                ready = []
            elif s == 1:
                outs = list(multiply((1, 2, 3), late, carry, ["emit"] * 3, tick - 1, outs))
                carry = None
            else:
                source = "sourced" if s == last_step else "carry"
                if s < last_step or final:
                    carry = multiply((0, 1, 2, 3), ready, carry, [source] + ["carry"] * 3, tick)[0]
                    late = []
                else:
                    carry = multiply((0,), ready, carry, [source], tick)[0]
                    late = ready
                ready = []
            ready = ready + arrived
        if final:
            res = multiply((0, 1, 2, 3), ready, carry, ["send"] + ["emit"] * 3, tick,
                           [None] + outs)
            return res[1], res[2], res[3], res[0][None]
        sent = multiply((0,), ready, carry, ["split"], tick)
        late = late + ready
        incoming = []
        for c in range(len(sent)):
            incoming.append(lax.ppermute(sent[c], "layer", [(i, i + 1) for i in range(layers - 1)]))


def plain_program(layers, transmission, reflection, receiver_map, midplane_map, traces, sources):
    incoming = sent = traces[0]
    outs = [[], [], []]
    for tick in range(sources.shape[1]):
        piece = lax.all_gather(incoming, "row", axis=0, tiled=True)
        total = jnp.dot(transmission[0], piece, preferred_element_type=jnp.float32)
        sent = (total + sources[0, tick].astype(jnp.float32)).astype(jnp.bfloat16)
        for out, w in zip(outs, (reflection, receiver_map, midplane_map)):
            out.append(jnp.dot(w[0], piece, preferred_element_type=jnp.float32).astype(jnp.bfloat16))
        incoming = lax.ppermute(sent, "layer", [(i, i + 1) for i in range(layers - 1)])
    return tuple(jnp.stack(o)[None] for o in outs) + (sent[None],)


def solution(mesh):
    layers, n = mesh.shape["layer"], mesh.shape["row"]

    def body(transmission, reflection, receiver_map, midplane_map, traces, sources):
        args = (transmission, reflection, receiver_map, midplane_map, traces, sources)
        if traces.shape[1] % 384 or n % 2 or n < 4:
            return plain_program(layers, *args)
        return sweep(layers, n, *args)

    wide = P("layer", "row", None)
    deep = P("layer", None, "row", None)
    return jax.shard_map(
        body,
        mesh=mesh,
        in_specs=(wide, wide, wide, wide, wide, deep),
        out_specs=(deep, deep, deep, wide),
        check_vma=False,
    )
```
